32 devices in a mesh: member: 2 (over y), gx: 4 (over x, core), gy: 4 (over z).
Axes of the slice: x: 2, y: 2, z: 4, core: 2. Of those that a mesh axis runs over, the one named last changes fastest.
Arguments:
- perm: float32 [64, 32, 512], P('member', 'gx', 'gy'), parts along dimension 0, may hold values from 0.2 to 5
- facies: int32 [64, 32, 512], P('member', 'gx', 'gy'), parts along dimension 0, may hold values from 0 to 3
- facies_porosity: float32 [4], replicated, may hold values from 0.15 to 0.35
- facies_mobility: float32 [4], replicated, may hold values from 0.5 to 2
- pressure: float32 [64, 32, 512], P('member', 'gx', 'gy'), parts along dimension 0, may hold values from -6 to 6
- saturation: float32 [64, 32, 512], P('member', 'gx', 'gy'), parts along dimension 0, may hold values from 0.1 to 0.9
- basis: float32 [64, 32, 512], P('member', 'gx', 'gy'), parts along dimension 0, may hold values from 0.75 to 1.33
- bx_map: int32 [64], P('member'), parts along dimension 0, may hold values from 0 to 3, as said below
- by_map: int32 [1024], P('member'), parts along dimension 0, may hold values from 0 to 63, as said below
- well_cells: int32 [64], P('member'), parts along dimension 0, may hold values from 0 to 16383
- well_rates: float32 [64], P('member'), parts along dimension 0, may hold values from -384 to 384
Outputs:
- new_pressure: float32 [64, 32, 512], P('member', 'gx', 'gy'), parts along dimension 0
- new_saturation: float32 [64, 32, 512], P('member', 'gx', 'gy'), parts along dimension 0
The draws below stay inside these ranges and needn't reach their ends.
There are 2 independent parts, one for each index of `member`. The reference program is written for one: setup_inputs(seed, part) draws one part's arguments, and reference() takes and returns one part's arrays. A program takes and returns all parts, laid end to end along the dimension named above; an argument that names none is the same for every part. Nothing has to cross between parts.
Inputs may be any that keep to these rules, and one draw needn't show every extreme that they name: `bx_map`: never falling; block 0 begins at position 0 and block k >= 1 begins at position 8 k + d with -2 <= d <= 2. `by_map`: never falling; block 0 begins at position 0 and block k >= 1 begins at position 8 k + d with -2 <= d <= 2.
All inputs are finite; a program needn't handle non-finite values.
Results may differ from the reference program's by a relative error of at most 0.0003.
Values sent between devices are 32-bit elements; how exact they have to be, the bound alone decides.
No kernel may reach another device: no remote copies, remote signals or barrier semaphores. Data moves between devices by JAX's collectives and lax.ppermute only.
A program may use at most 64 MiB of HBM per device.

```python
import math
import jax
import jax.numpy as jnp
from jax import lax

NZ = 32
BX = 8
BY = 8
BZ = 4
JIT = 2
NSWEEP = 3
NSUB = 4
NFAC = 4
NX = 32
NY = 512
NBX = 4
NBY = 64
NBZ = 8
WELLS = 32


def block_index(key, cells, blocks, length):
    shifts = jax.random.randint(key, (blocks - 1,), -JIT, JIT + 1, dtype=jnp.int32)
    starts = length * jnp.arange(1, blocks, dtype=jnp.int32) + shifts
    places = jnp.arange(cells, dtype=jnp.int32)
    return jnp.sum((places[:, None] >= starts[None, :]).astype(jnp.int32), axis=1).astype(jnp.int32)


def draw_bx_map(key, part):
    return block_index(jax.random.fold_in(key, 17), NX, NBX, BX)


def draw_by_map(key, part):
    return block_index(jax.random.fold_in(key, 29), NY, NBY, BY)


def place_ends(result, key, least, high):
    spot = [jax.random.randint(jax.random.fold_in(key, axis), (), 0, length) for axis, length in enumerate(result.shape)]
    widest = result.shape.index(max(result.shape))
    beside = spot[:widest] + [(spot[widest] + 1) % result.shape[widest]] + spot[widest + 1:]
    return result.at[tuple(spot)].set(least).at[tuple(beside)].set(high)


def level_of(rng, shape, split, least, largest):
    loudness = 1.0
    for dim, parts in split:
        heights = jax.random.uniform(jax.random.fold_in(jax.random.fold_in(rng, 6), dim), (parts,), jnp.float32, least / len(split), largest / len(split))
        loudness = loudness * jnp.repeat(jnp.exp(heights), shape[dim] // parts).reshape((-1,) + (1,) * (len(shape) - 1 - dim))
    return loudness


def scatter_about(key, dims, deviation, reach, shards=(), kind=jnp.bfloat16):
    factor_of = level_of(key, dims, shards, -0.22, 0.18) if shards else 1.0
    values = jax.random.normal(key, dims, jnp.float32) * deviation * factor_of
    return jnp.minimum(jnp.maximum(values, -reach), reach).astype(kind)


def setup_inputs(seed: int = 0, part: int = 0) -> dict:
    arg_keys = jax.random.split(jax.random.key(seed), 12)
    part_splits = jax.random.split(jax.random.fold_in(arg_keys[11], part), 12)
    return {
        "perm": jnp.clip(jnp.exp(math.log(5.0) - 3.218876 * jax.random.uniform(part_splits[0], (NZ, NX, NY), jnp.float32) ** level_of(part_splits[0], (NZ, NX, NY), ((1, 4), (2, 4)), -0.2, 0.2)), 0.2, 5.0),
        "facies": place_ends(jax.random.randint(part_splits[1], (NZ, NX, NY), 0, NFAC), jax.random.fold_in(part_splits[1], 1), 0, NFAC - 1).astype(jnp.int32),
        "facies_porosity": jnp.clip(jax.random.uniform(arg_keys[2], (NFAC,), jnp.float32, 0.15, 0.35), 0.15, 0.35),
        "facies_mobility": jnp.clip(jnp.exp(jax.random.uniform(arg_keys[3], (NFAC,), jnp.float32, math.log(0.5), math.log(2.0))), 0.5, 2.0),
        "pressure": scatter_about(part_splits[4], (NZ, NX, NY), 1.0, 6.0, ((1, 4), (2, 4)), jnp.float32),
        "saturation": jnp.clip(0.1 + 0.79999997 * jax.random.uniform(part_splits[5], (NZ, NX, NY), jnp.float32) ** level_of(part_splits[5], (NZ, NX, NY), ((1, 4), (2, 4)), -0.2, 0.2), 0.1, 0.9),
        "basis": jnp.clip(jnp.exp(math.log(1.33) - 0.57286105 * jax.random.uniform(part_splits[6], (NZ, NX, NY), jnp.float32) ** level_of(part_splits[6], (NZ, NX, NY), ((1, 4), (2, 4)), -0.2, 0.2)), 0.75, 1.33),
        "bx_map": draw_bx_map(jax.random.fold_in(jax.random.fold_in(arg_keys[11], part), 71), part),
        "by_map": draw_by_map(jax.random.fold_in(jax.random.fold_in(arg_keys[11], part), 71), part),
        "well_cells": place_ends(jax.random.randint(part_splits[9], (WELLS,), 0, NX * NY), jax.random.fold_in(part_splits[9], 1), 0, (NX * NY) - 1).astype(jnp.int32),
        "well_rates": scatter_about(part_splits[10], (WELLS,), (2 * NZ), 384.0, (), jnp.float32),
    }


viscosity_ratio = 4.0
vertical_factor = 0.1
storage_coefficient = 0.5
relaxation = 0.5
time_step = 0.005
highest = lax.Precision.HIGHEST


def lower(field, axis):
    return lax.slice_in_dim(field, 0, field.shape[axis] - 1, axis=axis)


def upper(field, axis):
    return lax.slice_in_dim(field, 1, field.shape[axis], axis=axis)


def pad_after(field, axis):
    widths = [(0, 1) if position == axis else (0, 0) for position in range(field.ndim)]
    return jnp.pad(field, widths)


def pad_before(field, axis):
    widths = [(1, 0) if position == axis else (0, 0) for position in range(field.ndim)]
    return jnp.pad(field, widths)


def harmonic(left, right):
    total = left + right
    return 2.0 * left * right / jnp.where(total > 0, total, 1.0)


def total_mobility(water_saturation):
    return water_saturation * water_saturation + (1.0 - water_saturation) * (1.0 - water_saturation) / viscosity_ratio


def fractional(water_saturation):
    wet = water_saturation * water_saturation
    return wet / (wet + (1.0 - water_saturation) * (1.0 - water_saturation) / viscosity_ratio)


def transmissibilities(mobility):
    return tuple((vertical_factor if axis == 0 else 1.0) * harmonic(lower(mobility, axis), upper(mobility, axis)) for axis in range(3))


def outflow(flows):
    total = 0.0
    for axis in range(3):
        total = total + pad_after(flows[axis], axis) - pad_before(flows[axis], axis)
    return total


def reference(perm, facies, facies_porosity, facies_mobility, pressure, saturation, basis, bx_map, by_map, well_cells, well_rates):
    porosity = facies_porosity[facies]
    mobility = perm * facies_mobility[facies] * total_mobility(saturation)
    trans = transmissibilities(mobility)
    column = jnp.zeros((NX * NY,), jnp.float32).at[well_cells].add(well_rates)
    source = jnp.broadcast_to((column / NZ).reshape(1, NX, NY), (NZ, NX, NY))
    pushes = tuple(trans[axis] * (lower(pressure, axis) - upper(pressure, axis)) for axis in range(3))
    residual = source - outflow(pushes)
    conductance = 0.0
    for axis in range(3):
        conductance = conductance + pad_after(trans[axis], axis) + pad_before(trans[axis], axis)
    cell_diagonal = basis * basis * (storage_coefficient * porosity + conductance)
    layer_blocks = jnp.arange(NZ, dtype=jnp.int32) // BZ
    same = ((layer_blocks[:-1] == layer_blocks[1:]).astype(jnp.float32).reshape(NZ - 1, 1, 1),
            (bx_map[:-1] == bx_map[1:]).astype(jnp.float32).reshape(1, NX - 1, 1),
            (by_map[:-1] == by_map[1:]).astype(jnp.float32).reshape(1, 1, NY - 1))
    couple = tuple(trans[axis] * lower(basis, axis) * upper(basis, axis) for axis in range(3))
    inner = 0.0
    for axis in range(3):
        inner = inner + pad_after(couple[axis] * same[axis], axis)
    onehot_x = (bx_map[:, None] == jnp.arange(NBX, dtype=jnp.int32)[None, :]).astype(jnp.float32)
    onehot_y = (by_map[:, None] == jnp.arange(NBY, dtype=jnp.int32)[None, :]).astype(jnp.float32)

    def to_blocks(field):
        stacked = field.reshape(NBZ, BZ, NX, NY).sum(axis=1)
        partial_sum = jnp.einsum('zab,ak->zkb', stacked, onehot_x, precision=highest)
        return jnp.einsum('zkb,bl->zkl', partial_sum, onehot_y, precision=highest)

    coarse_residual = to_blocks(basis * residual)
    coarse_diag = to_blocks(cell_diagonal - 2.0 * inner)
    crossing = []
    for axis in range(3):
        cut = couple[axis] * (1.0 - same[axis])
        crossing.append(to_blocks(pad_after(cut, axis)))
        crossing.append(to_blocks(pad_before(cut, axis)))

    def apply_coarse(estimate):
        applied = coarse_diag * estimate
        for axis in range(3):
            applied = applied - crossing[2 * axis] * pad_after(upper(estimate, axis), axis)
            applied = applied - crossing[2 * axis + 1] * pad_before(lower(estimate, axis), axis)
        return applied

    correction = relaxation * coarse_residual / coarse_diag
    for sweep in range(NSWEEP - 1):
        correction = correction + relaxation * (coarse_residual - apply_coarse(correction)) / coarse_diag
    fine_corr = jnp.einsum('zkl,ak->zal', correction, onehot_x, precision=highest)
    fine_corr = jnp.einsum('zal,bl->zab', fine_corr, onehot_y, precision=highest)
    fine_corr = jnp.repeat(fine_corr, BZ, axis=0)
    new_pressure = pressure + basis * fine_corr
    flows = tuple(trans[axis] * (lower(new_pressure, axis) - upper(new_pressure, axis)) for axis in range(3))
    water_saturation = saturation
    for substep in range(NSUB):
        frac = fractional(water_saturation)
        carried = tuple(jnp.where(flows[axis] > 0, lower(frac, axis), upper(frac, axis)) * flows[axis] for axis in range(3))
        change = jnp.maximum(source, 0.0) + jnp.minimum(source, 0.0) * frac - outflow(carried)
        water_saturation = water_saturation + time_step / porosity * change
    return new_pressure, water_saturation
```

```python
import jax
import jax.numpy as jnp
from jax import lax
from jax.experimental import pallas as pl
from jax.experimental.pallas import tpu as pltpu
from jax.sharding import PartitionSpec as P

BX = 8
BY = 8
BZ = 4
NSWEEP = 3
NSUB = 4

vertical_factor = 0.1
storage_coefficient = 0.5
relaxation = 0.5
time_step = 0.005
highest = lax.Precision.HIGHEST
f32 = jnp.float32
i32 = jnp.int32
SUB, LANES = 8, 128
REACH = NSWEEP
GROUP = 25
NT = (((1,), (1,)), ((), ()))
VM = pl.BlockSpec(memory_space=pltpu.VMEM)
SM = pl.BlockSpec(memory_space=pltpu.SMEM)


def iota(axis, shape=(SUB, LANES)):
    return lax.broadcasted_iota(i32, shape, axis)


def roll(v, shift, axis):
    size = v.shape[axis]
    shift = shift % size
    return v if shift == 0 else pltpu.roll(v, shift, axis)


def harmonic(a, b):
    total = a + b
    return 2.0 * a * b / jnp.where(total > 0, total, 1.0)


def spread(row):
    return jnp.broadcast_to(row, (SUB, LANES))


def fractional(w):
    wet = w * w
    return wet / (wet + (1.0 - w) * (1.0 - w) * 0.25)


def position():
    kx = lax.axis_index("gx")
    ky = lax.axis_index("gy")
    return kx, ky, kx % 2 == 0


def left_right(even, first, second):
    return jnp.where(even, first, second), jnp.where(even, second, first)


def prepare(perm, fac, press, sat, basis, fpor, fmob, mob_o, por_o, xa_o, xb_o, yf_o, yb_o):
    _, _, even = position()
    layers = perm.shape[0]
    lane = iota(1)
    for z in range(layers):
        kind = fac[z]
        por = jnp.full((SUB, LANES), fpor[0], f32)
        mul = jnp.full((SUB, LANES), fmob[0], f32)
        for level in range(1, fpor.shape[0]):
            here = kind == level
            por = jnp.where(here, fpor[level], por)
            mul = jnp.where(here, fmob[level], mul)
        w = sat[z]
        mob_o[z] = perm[z] * mul * (w * w + (1.0 - w) * (1.0 - w) * 0.25)
        por_o[z] = por
    for i, ref in enumerate((mob_o, press, basis)):
        low = ref[:, 0, :]
        high = ref[:, SUB - 1, :]
        xa_o[i * layers : (i + 1) * layers, :] = jnp.where(even, high, low)
        xb_o[i * layers : (i + 1) * layers, :] = jnp.where(even, low, high)
    for i, ref in enumerate((mob_o, press, basis, por_o, sat)):
        low = jnp.zeros((SUB, LANES), f32)
        high = low
        for z in range(layers):
            v = ref[z]
            here = (lane >> 2) == z
            low = jnp.where(here, roll(v, NSUB * z, 1), low)
            high = jnp.where(here, roll(v, NSUB * z + NSUB, 1), high)
        yf_o[i] = jnp.where(even, high, low)
        yb_o[i] = jnp.where(even, low, high)


def side_rows(kx, xt):
    row = iota(0)
    if xt == 0:
        return kx * SUB + row
    return kx * SUB + jnp.where(row < NSUB, row + SUB, row - SUB)


def side_columns(ky, side):
    l = iota(1) & (NSUB - 1)
    return ky * LANES + (-NSUB, 0, LANES - NSUB, LANES)[side] + l


def make_wells(full_x, full_y):
    def wells(cells, rates, col_o):
        kx, ky, _ = position()
        ids = []
        for side in range(-1, 4):
            y = ky * LANES + iota(1) if side < 0 else side_columns(ky, side)
            for xt in range(2):
                x = side_rows(kx, xt)
                ok = (x >= 0) & (x < full_x) & (y >= 0) & (y < full_y)
                ids.append(jnp.where(ok, x * full_y + y, -1))

        def step(k, cols):
            return tuple(
                col + jnp.where(i == cells[k], rates[k], 0.0) for i, col in zip(ids, cols)
            )

        cols = lax.fori_loop(
            0, cells.shape[0], step, tuple(jnp.zeros((SUB, LANES), f32) for _ in ids), unroll=4
        )
        layers = f32(col_o.shape[1])
        for i, col in enumerate(cols):
            col_o[i] = col

    return wells


def make_coarse(layers, n_gx, n_gy, full_x):
    zb_count = layers // BZ
    by_dev = LANES // BY
    bx_dev = SUB // BX

    def coarse(mob, por, press, basis, ra, rb, fr, br, bx, by, col, part_o, fields):
        kx, ky, even = position()
        row, lane = iota(0), iota(1)
        left_ok, right_ok = kx > 0, kx < n_gx - 1
        low_ok, high_ok = ky > 0, ky < n_gy - 1
        xl_all, xr_all = left_right(even, rb[...], ra[...])
        xl_all = jnp.where(left_ok, xl_all, 0.0)
        xr_all = jnp.where(right_ok, xr_all, 0.0)
        yl, yr = [], []
        for i in range(3):
            a, b = left_right(even, fr[i], br[i])
            yl.append(jnp.where(low_ok, a, 0.0))
            yr.append(jnp.where(high_ok, b, 0.0))
        x0 = kx * SUB
        xs = [bx[jnp.maximum(x0 - 1, 0)]]
        xs += [bx[x0 + r] for r in range(SUB)]
        xs += [bx[jnp.minimum(x0 + SUB, full_x - 1)]]

        def by_rows(offset):
            v = jnp.full((SUB, LANES), xs[offset], i32)
            for r in range(1, SUB):
                v = jnp.where(row == r, xs[offset + r], v)
            return v

        mx = by_rows(1)
        same_xp = mx == by_rows(2)
        same_xm = mx == by_rows(0)
        zero = jnp.zeros((1, LANES), i32)
        own, nxt, prv = zero, zero, zero
        for r in range(n_gy):
            line = by[r : r + 1, :]
            own = jnp.where(ky == r, line, own)
            nxt = jnp.where(ky + 1 == r, line, nxt)
            prv = jnp.where(ky - 1 == r, line, prv)
        own8, nxt8, prv8 = spread(own), spread(nxt), spread(prv)
        same_yp = own8 == jnp.where(lane == LANES - 1, roll(nxt8, -1, 1), roll(own8, -1, 1))
        same_ym = own8 == jnp.where(lane == 0, roll(prv8, 1, 1), roll(own8, 1, 1))
        src = col[0]
        first_row, last_row = row == 0, row == SUB - 1
        first_lane, last_lane = lane == 0, lane == LANES - 1

        def around(ref, i, z):
            v = ref[z]
            k = i * layers + z
            xp = jnp.where(last_row, spread(xr_all[k : k + 1, :]), roll(v, -1, 0))
            xm = jnp.where(first_row, spread(xl_all[k : k + 1, :]), roll(v, 1, 0))
            yp = jnp.where(last_lane, roll(yr[i], LANES - 1 - NSUB * z, 1), roll(v, -1, 1))
            ym = jnp.where(first_lane, roll(yl[i], -(NSUB * z + NSUB - 1), 1), roll(v, 1, 1))
            return v, (xp, xm, yp, ym)

        below = None
        for zb in range(zb_count):
            res = dia = cx = cy = cz = jnp.zeros((SUB, LANES), f32)
            for zz in range(BZ):
                z = zb * BZ + zz
                m, mn = around(mob, 0, z)
                p, pn = around(press, 1, z)
                b, bn = around(basis, 2, z)
                inflow = src
                cond = storage_coefficient * por[z]
                inner = jnp.zeros((SUB, LANES), f32)
                for j, same in enumerate((same_xp, same_xm, same_yp, same_ym)):
                    t = harmonic(m, mn[j])
                    inflow = inflow + t * (pn[j] - p)
                    cond = cond + t
                    c = t * b * bn[j]
                    inner = inner + jnp.where(same, c, 0.0)
                    if j == 0:
                        cx = cx + jnp.where(same, 0.0, c)
                    if j == 2:
                        cy = cy + jnp.where(same, 0.0, c)
                if below is not None:
                    push, t, c = below
                    inflow = inflow + push
                    cond = cond + t
                    if zz:
                        inner = inner + c
                if z + 1 < layers:
                    t = vertical_factor * harmonic(m, mob[z + 1])
                    push = t * (p - press[z + 1])
                    c = t * b * basis[z + 1]
                    inflow = inflow - push
                    cond = cond + t
                    if zz + 1 < BZ:
                        inner = inner + c
                    else:
                        cz = cz + c
                    below = (push, t, c)
                res = res + b * inflow
                dia = dia + (b * b * cond - inner)
            for i, v in enumerate((res, dia, cx, cy, cz)):
                fields[i, zb * SUB : (zb + 1) * SUB, :] = v
        out = iota(0, (LANES, LANES))
        target = jnp.broadcast_to(own, (LANES, LANES)) - ky * by_dev + REACH
        sums = jnp.zeros((zb_count * SUB, LANES), f32)
        for i in range(5):
            pick = jnp.where(out - GROUP * i == target, 1.0, 0.0).astype(f32)
            sums = sums + lax.dot_general(
                fields[i], pick, NT, precision=highest, preferred_element_type=f32
            )
        shape = (3 * zb_count, zb_count * SUB)
        r2, c2 = iota(0, shape), iota(1, shape)
        xpos = c2 % SUB
        mapped = jnp.full(shape, xs[1], i32)
        for r in range(1, SUB):
            mapped = jnp.where(xpos == r, xs[1 + r], mapped)
        hit = (r2 % zb_count == c2 // SUB) & (mapped == kx * bx_dev - 1 + r2 // zb_count)
        gather = jnp.where(hit, 1.0, 0.0).astype(f32)
        part_o[...] = jnp.dot(gather, sums, precision=highest, preferred_element_type=f32)

    return coarse


def pair_up(u, v):
    row = iota(0)
    v = roll(v, NSUB, 0)
    return jnp.where(row >= NSUB, u, v), jnp.where(row < NSUB, u, v)


def edge_packs(even, i, fr, br, yf, yb, low_ok, high_ok):
    far_low, far_high = left_right(even, fr[i], br[i])
    near_high, near_low = left_right(even, yf[i], yb[i])
    return (
        jnp.where(low_ok, far_low, 0.0),
        near_low,
        near_high,
        jnp.where(high_ok, far_high, 0.0),
    )


def make_bulk(layers, n_gy):
    half = layers // 2

    def bulk(mob, press, basis, por, sat, fr, br, yf, yb, a_o, b_o):
        _, ky, even = position()
        low_ok, high_ok = ky > 0, ky < n_gy - 1
        for i, ref in enumerate((mob, press, basis, por, sat)):
            pl_, ol, or_, pr = edge_packs(even, i, fr, br, yf, yb, low_ok, high_ok)
            pairs = [(ref[k], ref[k + half]) for k in range(half)] + [(pl_, ol), (or_, pr)]
            for k, (u, v) in enumerate(pairs):
                high, low = pair_up(u, v)
                a_o[i * (half + 2) + k] = jnp.where(even, high, low)
                b_o[i * (half + 2) + k] = jnp.where(even, low, high)

    return bulk


def make_join(n_gy):
    by_dev = LANES // BY

    def join(part, fr, br, out):
        _, ky, even = position()
        low, high = left_right(even, fr[...], br[...])
        lane = iota(1, part.shape)
        w = lane
        for g in range(1, 5):
            w = w - jnp.where(lane >= GROUP * g, GROUP, 0)
        span = by_dev + 2 * REACH
        take_high = (w >= span - REACH - 1) & (w < span) & (ky < n_gy - 1)
        take_low = (w < REACH + 1) & (ky > 0)
        out[...] = (
            part[...]
            + jnp.where(take_high, roll(high, by_dev, 1), 0.0)
            + jnp.where(take_low, roll(low, -by_dev, 1), 0.0)
        )

    return join


def shift_x(t0, t1, last_row):
    a, b = roll(t0, -1, 0), roll(t1, -1, 0)
    return jnp.where(last_row, b, a), jnp.where(last_row, a, b)


def back_x(t0, t1, first_row):
    a, b = roll(t0, 1, 0), roll(t1, 1, 0)
    return jnp.where(first_row, b, a), jnp.where(first_row, a, b)


def pack_up(packs, l):
    last = l == NSUB - 1
    moved = [roll(v, -1, 1) for v in packs]
    moved[0] = jnp.where(last, roll(packs[1], NSUB - 1, 1), moved[0])
    moved[2] = jnp.where(last, roll(packs[3], NSUB - 1, 1), moved[2])
    return moved


def pack_down(packs, l):
    first = l == 0
    moved = [roll(v, 1, 1) for v in packs]
    moved[1] = jnp.where(first, roll(packs[0], 1 - NSUB, 1), moved[1])
    moved[3] = jnp.where(first, roll(packs[2], 1 - NSUB, 1), moved[3])
    return moved


def make_trans(layers, n_gx, n_gy):
    half = layers // 2

    def trans(mob, por, ra, rb, fr, br, yf, yb, t_o, s_o, halo_o, tp_o, sp_o, pk_o, mx):
        kx, ky, even = position()
        row, lane = iota(0), iota(1)
        l = lane & (NSUB - 1)
        last_row = row == SUB - 1
        low_ok, high_ok = ky > 0, ky < n_gy - 1
        left_ok, right_ok = kx > 0, kx < n_gx - 1
        low_half = row < NSUB
        packs = []
        for i in range(5):
            base = i * (half + 2)
            mine = edge_packs(even, i, fr, br, yf, yb, low_ok, high_ok)
            theirs = []
            for k in range(half + 2):
                a, b = ra[base + k], rb[base + k]
                high, low = left_right(even, b, a)
                low = jnp.where(right_ok, low, 0.0)
                high = jnp.where(left_ok, high, 0.0)
                first = jnp.where(low_half, low, high)
                second = roll(jnp.where(low_half, high, low), NSUB, 0)
                if k < half:
                    for z, v in ((k, first), (k + half, second)):
                        if i == 0:
                            mx[z] = v
                        elif i == 3:
                            s_o[z, 1] = time_step / jnp.where(v > 0, v, 1.0)
                        else:
                            halo_o[(None, 0, 1, None, 2)[i], z] = v
                else:
                    theirs += [first, second]
            packs.append((mine, theirs))
        for i, j in ((1, 0), (2, 1), (4, 2)):
            for xt in range(2):
                for side in range(4):
                    pk_o[j, xt * 4 + side] = packs[i][xt][side]
        for xt in range(2):
            for side in range(4):
                v = packs[3][xt][side]
                sp_o[xt * 4 + side] = time_step / jnp.where(v > 0, v, 1.0)
        m = packs[0]
        for side in range(4):
            n0, n1 = shift_x(m[0][side], m[1][side], last_row)
            tp_o[0, side] = harmonic(m[0][side], n0)
            tp_o[0, 4 + side] = harmonic(m[1][side], n1)
        for xt in range(2):
            up = pack_up(m[xt], l)
            for side in range(4):
                tp_o[1, xt * 4 + side] = harmonic(m[xt][side], up[side])
                tz = vertical_factor * harmonic(m[xt][side], roll(m[xt][side], -NSUB, 1))
                tp_o[2, xt * 4 + side] = jnp.where(lane < LANES - NSUB, tz, 0.0)
        for z in range(layers):
            s_o[z, 0] = time_step / por[z]
            m0, m1 = mob[z], mx[z]
            n0, n1 = shift_x(m0, m1, last_row)
            t_o[0, z, 0] = harmonic(m0, n0)
            t_o[0, z, 1] = harmonic(m1, n1)
            t_o[1, z, 0] = harmonic(m0, roll(m0, -1, 1))
            t_o[1, z, 1] = harmonic(m1, roll(m1, -1, 1))
            if z + 1 < layers:
                t_o[2, z, 0] = vertical_factor * harmonic(m0, mob[z + 1])
                t_o[2, z, 1] = vertical_factor * harmonic(m1, mx[z + 1])

    return trans


def coefficients(s, src, out_p, flows_p, flows_m):
    outgoing = 0.0
    gains = []
    for fp, fm in zip(flows_p, flows_m):
        lost = jnp.maximum(fp, 0.0)
        gains.append(s * (lost - fp))
        won = jnp.maximum(fm, 0.0)
        gains.append(s * won)
        outgoing = outgoing + lost + (won - fm)
    keep = s * (jnp.minimum(src, 0.0) - outgoing)
    return gains, keep, s * jnp.maximum(src, 0.0)


def make_finish(layers, n_gx, n_gy, full_x, full_y, offsets):
    zb_count = layers // BZ
    by_dev = LANES // BY
    bx_dev = SUB // BX
    span = by_dev + 2 * REACH
    slots = 2 * REACH + 1

    def finish(*refs):
        (press, sat, basis, t, s, halo, tp, sp, pk, col, bx, bys, by, part), refs = refs[:14], refs[14:]
        moved, refs = refs[: len(offsets)], refs[len(offsets) :]
        np_o, w_o, est_s, np_s, cf, wx, fr_s, cp, wp, fp = refs
        kx, ky, even = position()
        row, lane = iota(0), iota(1)
        l = lane & (NSUB - 1)
        first_row, last_row = row == 0, row == SUB - 1
        first_lane, last_lane = lane == 0, lane == LANES - 1
        zeros = jnp.zeros((SUB, LANES), f32)

        window = [zeros] * slots
        for o in range(-REACH - 1, REACH + 2):
            if o == 0:
                source, ok = part, None
            elif (-o) % n_gx in offsets:
                source = moved[offsets.index((-o) % n_gx)]
                ok = (kx + o >= 0) & (kx + o < n_gx)
            else:
                continue
            for q in range(3):
                slot = o + q - 1 + REACH
                if 0 <= slot < slots:
                    v = source[q * zb_count : (q + 1) * zb_count, :]
                    if ok is not None:
                        v = jnp.where(ok, v, 0.0)
                    window[slot] = window[slot] + v
        res = window
        dia, cx, cy, cz = ([roll(v, -GROUP * g, 1) for v in window] for g in range(1, 5))
        dia = [jnp.where(v > 0, v, 1.0) for v in dia]
        inside = lane < span
        est = [jnp.where(inside, relaxation * r / d, 0.0) for r, d in zip(res, dia)]
        for sweep in range(1, NSWEEP):
            new = list(est)
            for j in range(sweep, slots - sweep):
                e = est[j]
                applied = dia[j] * e
                applied = applied - cz[j] * roll(e, -1, 0) - roll(cz[j] * e, 1, 0)
                applied = applied - cx[j] * est[j + 1] - cx[j - 1] * est[j - 1]
                applied = applied - cy[j] * roll(e, -1, 1) - roll(cy[j] * e, 1, 1)
                e = e + relaxation * (res[j] - applied) / dia[j]
                new[j] = jnp.where(inside, e, 0.0)
            est = new
        mid = jnp.concatenate(est[REACH - 1 : REACH + 2], axis=0)

        own = jnp.zeros((1, LANES), i32)
        for r in range(n_gy):
            own = jnp.where(ky == r, by[r : r + 1, :], own)
        shape = (LANES, LANES)
        out = iota(0, shape)
        base = ky * by_dev - REACH
        pick = jnp.where(out == jnp.broadcast_to(own, shape) - base, 1.0, 0.0).astype(f32)
        est_s[...] = jnp.dot(mid, pick, precision=highest, preferred_element_type=f32)
        marks = []
        for xt in range(2):
            v = jnp.zeros((SUB, LANES), i32)
            for r in range(SUB):
                x = kx * SUB + (r if xt == 0 else (r + SUB if r < NSUB else r - SUB))
                v = jnp.where(row == r, bx[jnp.clip(x, 0, full_x - 1)], v)
            v = v - (kx * bx_dev - 1)
            marks.append((v == 0, v == 1))

        def by_column(xt, rows):
            first, second = marks[xt]
            return jnp.where(first, rows[0], jnp.where(second, rows[1], rows[2]))

        pack_corr = [[None] * 4 for _ in range(2)]
        for side in range(4):
            y0 = ky * LANES + (-NSUB, 0, LANES - NSUB, LANES)[side]
            v = jnp.zeros((1, LANES), i32)
            for k in range(NSUB):
                v = jnp.where(l[0:1, :] == k, bys[jnp.clip(y0 + k, 0, full_y - 1)], v)
            pick = jnp.where(out == jnp.broadcast_to(v, shape) - base, 1.0, 0.0).astype(f32)
            wide = jnp.dot(mid, pick, precision=highest, preferred_element_type=f32)
            rows = []
            for q in range(3):
                piece = wide[q * zb_count : (q + 1) * zb_count, :]
                piece = jnp.where(row == lane // (NSUB * BZ), piece, 0.0)
                rows.append(spread(jnp.sum(piece, axis=0, keepdims=True)))
            for xt in range(2):
                pack_corr[xt][side] = by_column(xt, rows)

        np_p = [
            [pk[0, xt * 4 + i] + pk[1, xt * 4 + i] * pack_corr[xt][i] for i in range(4)]
            for xt in range(2)
        ]
        fx_p = [[None] * 4 for _ in range(2)]
        fxm_p = [[None] * 4 for _ in range(2)]
        for i in range(4):
            n = shift_x(np_p[0][i], np_p[1][i], last_row)
            for xt in range(2):
                fx_p[xt][i] = tp[0, xt * 4 + i] * (np_p[xt][i] - n[xt])
            fxm_p[0][i], fxm_p[1][i] = back_x(fx_p[0][i], fx_p[1][i], first_row)
        high_flow, low_flow = [], []
        for xt in range(2):
            up = pack_up(np_p[xt], l)
            fy = [tp[1, xt * 4 + i] * (np_p[xt][i] - up[i]) for i in range(4)]
            fym = pack_down(fy, l)
            high_flow.append(fy[2])
            low_flow.append(fy[0])
            for i in range(4):
                k = xt * 4 + i
                fz = tp[2, k] * (np_p[xt][i] - roll(np_p[xt][i], -NSUB, 1))
                fzm = roll(fz, NSUB, 1)
                gains, keep, add = coefficients(
                    sp[k], col[2 + 2 * i + xt], None, (fx_p[xt][i], fy[i], fz), (fxm_p[xt][i], fym[i], fzm)
                )
                for g, v in enumerate(gains + [keep, add]):
                    cp[g, k] = v
                wp[k] = pk[2, k]
                fp[k] = fractional(pk[2, k])

        for zb in range(zb_count):
            rows = [spread(est_s[q * zb_count + zb : q * zb_count + zb + 1, :]) for q in range(3)]
            corr = [by_column(xt, rows) for xt in range(2)]
            for zz in range(BZ):
                z = zb * BZ + zz
                v = press[z] + basis[z] * corr[0]
                np_o[z] = v
                np_s[z] = halo[0, z] + halo[1, z] * corr[1]

        below = [zeros, zeros]
        for z in range(layers):
            v = (np_o[z], np_s[z])
            n = shift_x(v[0], v[1], last_row)
            fx = [t[0, z, xt] * (v[xt] - n[xt]) for xt in range(2)]
            fxm = back_x(fx[0], fx[1], first_row)
            for xt in range(2):
                fy = t[1, z, xt] * (v[xt] - roll(v[xt], -1, 1))
                fy = jnp.where(last_lane, roll(high_flow[xt], LANES - NSUB - NSUB * z, 1), fy)
                fym = jnp.where(
                    first_lane, roll(low_flow[xt], -(NSUB * z + NSUB - 1), 1), roll(fy, 1, 1)
                )
                if z + 1 < layers:
                    fz = t[2, z, xt] * (v[xt] - (np_o, np_s)[xt][z + 1])
                else:
                    fz = zeros
                gains, keep, add = coefficients(
                    s[z, xt], col[xt], None, (fx[xt], fy, fz), (fxm[xt], fym, below[xt])
                )
                below[xt] = fz
                for g, c in enumerate(gains + [keep, add]):
                    cf[g, z, xt] = c
                w = sat[z] if xt == 0 else halo[2, z]
                wx[z, xt] = w
                fr_s[0, z, xt] = fractional(w)

        def advance(w, c, f, xp, xm, yp, ym, zp, zm):
            change = c(0) * xp + c(1) * xm + c(2) * yp + c(3) * ym
            if zp is not None:
                change = change + c(4) * zp
            if zm is not None:
                change = change + c(5) * zm
            return w + (change + (c(6) * f + c(7)))

        for sub in range(NSUB):
            last = sub == NSUB - 1
            fin, fout = sub % 2, (sub + 1) % 2
            fpk = [[fp[xt * 4 + i] for i in range(4)] for xt in range(2)]
            high_f = [fpk[xt][3] for xt in range(2)]
            low_f = [fpk[xt][0] for xt in range(2)]
            if not last:
                xps = [shift_x(fpk[0][i], fpk[1][i], last_row) for i in range(4)]
                xms = [back_x(fpk[0][i], fpk[1][i], first_row) for i in range(4)]
                for xt in range(2):
                    up, down = pack_up(fpk[xt], l), pack_down(fpk[xt], l)
                    for i in range(4):
                        k = xt * 4 + i
                        f = fpk[xt][i]
                        w = advance(
                            wp[k], lambda g: cp[g, k], f, xps[i][xt], xms[i][xt], up[i], down[i],
                            roll(f, -NSUB, 1), roll(f, NSUB, 1),
                        )
                        wp[k] = w
                        fp[k] = fractional(w)
            for z in range(layers):
                f = (fr_s[fin, z, 0], fr_s[fin, z, 1])
                xp = shift_x(f[0], f[1], last_row)
                xm = back_x(f[0], f[1], first_row)
                for xt in range(1 if last else 2):
                    yp = jnp.where(
                        last_lane, roll(high_f[xt], LANES - 1 - NSUB * z, 1), roll(f[xt], -1, 1)
                    )
                    ym = jnp.where(
                        first_lane, roll(low_f[xt], -(NSUB * z + NSUB - 1), 1), roll(f[xt], 1, 1)
                    )
                    zp = fr_s[fin, z + 1, xt] if z + 1 < layers else None
                    zm = fr_s[fin, z - 1, xt] if z > 0 else None
                    w = advance(
                        wx[z, xt], lambda g: cf[g, z, xt], f[xt], xp[xt], xm[xt], yp, ym, zp, zm
                    )
                    if last:
                        w_o[z] = w
                    else:
                        wx[z, xt] = w
                        fr_s[fout, z, xt] = fractional(w)

    return finish


def call(kernel, name, out, specs, scratch=()):
    return pl.pallas_call(
        kernel,
        name=name,
        out_shape=tuple(jax.ShapeDtypeStruct(shape, f32) for shape in out),
        in_specs=specs,
        out_specs=tuple(VM for _ in out),
        scratch_shapes=[pltpu.VMEM(shape, f32) for shape in scratch],
    )


def make_body(n_gx, n_gy):
    axes = ("gx", "gy")

    def moves(rule):
        return [
            (x * n_gy + y, (lambda a, b: a * n_gy + b)(*rule(x, y)))
            for x in range(n_gx)
            for y in range(n_gy)
        ]

    def snake(x, y, up):
        if up:
            return (x, y + 1) if y + 1 < n_gy else (x ^ 1, y)
        return (x, y - 1) if y > 0 else (x ^ 1, y)

    def across(x, y):
        if x % 2 == 1 and x + 1 < n_gx:
            return (x + 1, y)
        if x % 2 == 0 and x > 0:
            return (x - 1, y)
        return (x, y ^ 1)

    forward = moves(lambda x, y: snake(x, y, x % 2 == 0))
    backward = moves(lambda x, y: snake(x, y, x % 2 == 1))
    pair_a = moves(lambda x, y: (x ^ 1, y))
    pair_b = moves(across)
    offsets = sorted({o % n_gx for o in range(-REACH - 1, REACH + 2)} - {0})

    def body(
        perm, facies, facies_porosity, facies_mobility, pressure, saturation, basis,
        bx_map, by_map, well_cells, well_rates,
    ):
        layers, width_x, width_y = pressure.shape
        assert (width_x, width_y) == (SUB, LANES) and layers * NSUB == LANES
        full_x, full_y = bx_map.shape[0], by_map.shape[0]
        zb_count = layers // BZ
        half = layers // 2
        tile = (SUB, LANES)
        by_rows = by_map.reshape(n_gy, LANES)
        move = lambda v, pairs: lax.ppermute(v, axes, pairs)

        mob, por, xa, xb, yf, yb = call(
            prepare, "prepare",
            [(layers,) + tile] * 2 + [(3 * layers, LANES)] * 2 + [(5,) + tile] * 2,
            [VM] * 5 + [SM] * 2,
        )(perm, facies, pressure, saturation, basis, facies_porosity, facies_mobility)
        ra, rb = move(xa, pair_a), move(xb, pair_b)
        fr, br = move(yf, forward), move(yb, backward)

        (col,) = call(make_wells(full_x, full_y), "wells", [(10,) + tile], [SM] * 2)(
            well_cells, well_rates / layers
        )
        (part,) = call(
            make_coarse(layers, n_gx, n_gy, full_x), "coarse", [(3 * zb_count, LANES)],
            [VM] * 8 + [SM, VM, VM], [(5, zb_count * SUB, LANES)],
        )(mob, por, pressure, basis, ra, rb, fr, br, bx_map, by_rows, col)
        pf, pb = move(part, forward), move(part, backward)
        ba, bb = call(
            make_bulk(layers, n_gy), "bulk", [(5 * (half + 2),) + tile] * 2, [VM] * 9
        )(mob, pressure, basis, por, saturation, fr, br, yf, yb)
        (joined,) = call(make_join(n_gy), "join", [(3 * zb_count, LANES)], [VM] * 3)(part, pf, pb)
        moved = [
            lax.ppermute(joined, "gx", [(i, (i + d) % n_gx) for i in range(n_gx)]) for d in offsets
        ]
        qa, qb = move(ba, pair_a), move(bb, pair_b)
        t, s, halo, tp, sp, pk = call(
            make_trans(layers, n_gx, n_gy), "trans",
            [(3, layers, 2) + tile, (layers, 2) + tile, (3, layers) + tile, (3, 8) + tile,
             (8,) + tile, (3, 8) + tile],
            [VM] * 8, [(layers,) + tile],
        )(mob, por, qa, qb, fr, br, yf, yb)
        return call(
            make_finish(layers, n_gx, n_gy, full_x, full_y, offsets), "finish",
            [(layers,) + tile] * 2,
            [VM] * 10 + [SM, SM, VM, VM] + [VM] * len(offsets),
            [(3 * zb_count, LANES), (layers,) + tile, (8, layers, 2) + tile, (layers, 2) + tile,
             (2, layers, 2) + tile, (8, 8) + tile, (8,) + tile, (8,) + tile],
        )(pressure, saturation, basis, t, s, halo, tp, sp, pk, col, bx_map, by_map, by_rows, joined, *moved)

    return body


def solution(mesh):
    cells = P("member", "gx", "gy")
    each = P("member")
    return jax.shard_map(
        make_body(mesh.shape["gx"], mesh.shape["gy"]),
        mesh=mesh,
        in_specs=(cells, cells, P(), P(), cells, cells, cells, each, each, each, each),
        out_specs=(cells, cells),
        check_vma=False,
    )
```
